128 devices in a mesh: stream: 4 (over x), cross: 32 (over y, z, core).
Axes of the slice: x: 4, y: 4, z: 4, core: 2. Of those that a mesh axis runs over, the one named last changes fastest.
Arguments:
- velocity: bfloat16 [128, 3, 48, 256, 128], P(None, None, 'stream', 'cross'), may hold values from -40 to 40, as said below
- metric_x: float32 [48], P('stream'), may hold values from 0.5 to 2
- metric_y: float32 [256], P('cross'), may hold values from 0.5 to 2
- metric_z: float32 [128], replicated, may hold values from 0.5 to 2
Outputs:
- modes: bfloat16 [128, 4, 48, 256, 128], P(None, None, 'stream', 'cross')
- factor: float32 [128, 128], replicated
The draws below stay inside these ranges and needn't reach their ends.
Inputs may be any that keep to these rules, and one draw needn't show every extreme that they name: velocity snapshots share a common part across snapshots.
All inputs are finite; a program needn't handle non-finite values.
Results may differ from the reference program's by a relative error of at most 0.0023.
The reference program's roundings to bfloat16 on the way count: a program that leaves them out, or rounds other values in their place, can miss the bound.
Values may be sent and summed in bfloat16 or wider, within the bound.
A program may use at most 128 MiB of HBM per device.

```python
import math
import jax
import jax.numpy as jnp
from jax import lax

SNAP = 128
NZ = 128
NX = 48
NY = 256


def draw_velocity(key, part):
    key_noise, key_common, key_rough = jax.random.split(jax.random.fold_in(key, 17), 3)
    shape = (SNAP, 3, NX, NY, NZ)
    common_shape = (1, 3, NX, NY, NZ)
    noise = jax.random.normal(key_noise, shape, jnp.float32)
    common = jax.random.normal(key_common, common_shape, jnp.float32)
    weight = 1.5
    rough = 2.0 ** jax.random.uniform(key_rough, common_shape, jnp.float32, -1.0, 1.0)
    rising = 10.0 ** (0.8 * jnp.arange(NY, dtype=jnp.float32) / NY)
    value = (weight * common + 0.5 * noise * rising[None, None, None, :, None]) * rough
    return jnp.clip(value, -40.0, 40.0).astype(jnp.bfloat16)


def levels(rng, extent, shards, least, top_value):
    def one(dim, blocks):
        draws = jax.random.uniform(jax.random.fold_in(jax.random.fold_in(rng, 6), dim), (blocks,), jnp.float32, least / len(shards), top_value / len(shards))
        return jnp.repeat(jnp.exp(draws), extent[dim] // blocks).reshape((-1,) + (1,) * (len(extent) - dim - 1))

    gain = one(*shards[0])
    for cut in shards[1:]:
        gain = gain * one(*cut)
    return gain


def setup_inputs(seed: int = 0) -> dict:
    seeds = jax.random.split(jax.random.key(seed), 5)
    return {
        "velocity": draw_velocity(jax.random.fold_in(seeds[4], 71), 0),
        "metric_x": jnp.clip(jnp.exp(math.log(2.0) - 1.3862944 * jax.random.uniform(seeds[1], (NX,), jnp.float32) ** levels(seeds[1], (NX,), ((0, 4),), -0.2, 0.2)), 0.5, 2.0),
        "metric_y": jnp.clip(jnp.exp(math.log(2.0) - 1.3862944 * jax.random.uniform(seeds[2], (NY,), jnp.float32) ** levels(seeds[2], (NY,), ((0, 32),), -0.2, 0.2)), 0.5, 2.0),
        "metric_z": jnp.clip(jnp.exp(jax.random.uniform(seeds[3], (NZ,), jnp.float32, math.log(0.5), math.log(2.0))), 0.5, 2.0),
    }


def central(padded, axis):
    count = padded.shape[axis] - 4

    def part_at(offset):
        return lax.slice_in_dim(padded, offset, offset + count, axis=axis)
    return (8.0 * (part_at(3) - part_at(1)) - (part_at(4) - part_at(0))) / 12.0

def fields(block, metric_x, metric_y, metric_z):
    values = block.astype(jnp.float32)

    def deriv_x(field):
        return central(field[:, :, 2:-2, :], 1) * metric_x[:, None, None]

    def deriv_y(field):
        return central(field[:, 2:-2, :, :], 2) * metric_y[:, None]

    def deriv_z(field):
        interior = field[:, 2:-2, 2:-2, :]
        return central(jnp.pad(interior, ((0, 0), (0, 0), (0, 0), (2, 2))), 3) * metric_z
    stream_vel = values[:, 0]
    cross_vel = values[:, 1]
    span_vel = values[:, 2]
    vort_x = deriv_y(span_vel) - deriv_z(cross_vel)
    vort_y = deriv_z(stream_vel) - deriv_x(span_vel)
    vort_z = deriv_x(cross_vel) - deriv_y(stream_vel)
    dilatation = deriv_x(stream_vel) + deriv_y(cross_vel) + deriv_z(span_vel)
    return jnp.stack([vort_x, vort_y, vort_z, dilatation], axis=1).astype(jnp.bfloat16)

def inner_products(flat):
    return lax.dot_general(flat.astype(jnp.float32), flat.astype(jnp.float32), (((1,), (1,)), ((), ())), preferred_element_type=jnp.float32)

def reference(velocity, metric_x, metric_y, metric_z):
    blocks = velocity.reshape(SNAP // 8, 8, 3, NX, NY, NZ)

    def one_block(block):
        padded = jnp.pad(block, ((0, 0), (0, 0), (2, 2), (2, 2), (0, 0)))
        return fields(padded, metric_x, metric_y, metric_z)
    flat = lax.map(one_block, blocks).reshape(SNAP, 4 * NX * NY * NZ)
    scale = 1.0 / (4.0 * NX * NY * NZ)
    gram = inner_products(flat) * scale
    lower = jnp.linalg.cholesky(gram)
    identity = jnp.eye(SNAP, dtype=jnp.float32)
    inverse = jax.scipy.linalg.solve_triangular(lower, identity, lower=True)
    basis = jnp.dot(inverse.astype(jnp.bfloat16).astype(jnp.float32), flat.astype(jnp.float32), preferred_element_type=jnp.float32).astype(jnp.bfloat16)
    return (basis.reshape(SNAP, 4, NX, NY, NZ), lower)
```

```python
import functools

import jax
import jax.numpy as jnp
from jax import lax
from jax.experimental import pallas as pl
from jax.experimental.pallas import tpu as pltpu
from jax.sharding import PartitionSpec as P

MESH = pl.DeviceIdType.MESH
F32 = jnp.float32
BF16 = jnp.bfloat16
VMEM_LIMIT = 60 * 1024 * 1024
PANEL = 8


def gram_kernel(
    sizes, vel, mx, my, mz, sz, x_out, gram_out,
    raw, tiles, stack, wide, dz, acc, half, part, whole,
    load_sem, out_sem, xs_sem, xr_sem, xs2_sem, xr2_sem, ys_sem, yr_sem,
    cs_sem, cr_sem, as_sem, ar_sem, fs_sem, fr_sem,
):
    nx, ny, nz = sizes
    comps, xp, yp, snaps, cz = tiles.shape
    xl, yl = xp - 4, yp - 4
    nc = ny * nz * 2
    sx = lax.axis_index("stream")
    cr = lax.axis_index("cross")
    core = cr % 2
    iz = (cr // 2) % nz
    iy = cr // (2 * nz)
    rows = snaps // 2

    def x_peer(k):
        return ((sx + k) % nx, cr)

    def y_peer(k):
        return (sx, (((iy + k) % ny) * nz + iz) * 2 + core)

    def z_peer(k):
        return (sx, (iy * nz + (iz + k) % nz) * 2 + core)

    twin = (sx, cr + 1 - 2 * core)
    up = (sx, (cr + 1) % nc)
    down = (sx, (cr + nc - 1) % nc)

    def load(b):
        c, x = b % comps, (b // comps + xl - 2) % xl
        return pltpu.make_async_copy(vel.at[:, c, x], raw.at[b], load_sem.at[b])

    @pl.loop(0, comps * xl)
    def _(b):
        load(b).start()

    barrier = pltpu.get_barrier_semaphore()
    peers = [x_peer(k) for k in range(1, nx)] + [y_peer(k) for k in range(1, ny)]
    peers += [z_peer(k) for k in range(1, nz)] + [twin, up, down]
    for peer in peers:
        pl.semaphore_signal(barrier, inc=1, device_id=peer, device_id_type=MESH)

    @pl.when(sx == 0)
    def _():
        tiles[:, 0:2, 2 : yl + 2] = jnp.zeros((comps, 2, yl, snaps, cz), BF16)

    @pl.when(sx == nx - 1)
    def _():
        tiles[:, xl + 2 : xl + 4, 2 : yl + 2] = jnp.zeros((comps, 2, yl, snaps, cz), BF16)

    @pl.when(cr == 0)
    def _():
        tiles[:, 2 : xl + 2, 0:2] = jnp.zeros((comps, xl, 2, snaps, cz), BF16)

    @pl.when(cr == nc - 1)
    def _():
        tiles[:, 2 : xl + 2, yl + 2 : yl + 4] = jnp.zeros((comps, xl, 2, snaps, cz), BF16)

    pl.semaphore_wait(barrier, len(peers))

    def turn(b):
        c, x = b % comps, (b // comps + xl - 2) % xl
        load(b).wait()
        wide[...] = raw[b].astype(F32).reshape(snaps * yl, cz)
        for y in range(yl):
            tiles[c, x + 2, y + 2] = wide[pl.ds(y, snaps, stride=yl), :].astype(BF16)

    def remote(src, dst, send, recv, peer):
        return pltpu.make_async_remote_copy(
            src_ref=src, dst_ref=dst, send_sem=send, recv_sem=recv,
            device_id=peer, device_id_type=MESH,
        )

    right = ((sx + 1) % nx, cr)
    left = ((sx + nx - 1) % nx, cr)
    inner = pl.ds(2, yl)

    def x_right(c, r):
        return remote(
            tiles.at[c, xl + r, inner], tiles.at[c, r, inner],
            xs_sem.at[0, c, r], xr_sem.at[0, c, r], right,
        )

    def x_left(c, r):
        return remote(
            tiles.at[c, 2 + r, inner], tiles.at[c, xl + 2 + r, inner],
            xs_sem.at[1, c, r], xr_sem.at[1, c, r], left,
        )

    last = comps - 1

    def x_right_last(y):
        return remote(
            tiles.at[last, pl.ds(xl, 2), y + 2], tiles.at[last, pl.ds(0, 2), y + 2],
            xs2_sem.at[0, y], xr2_sem.at[0, y], right,
        )

    def x_left_last(y):
        return remote(
            tiles.at[last, pl.ds(2, 2), y + 2], tiles.at[last, pl.ds(xl + 2, 2), y + 2],
            xs2_sem.at[1, y], xr2_sem.at[1, y], left,
        )

    def y_up(c, x):
        return remote(
            tiles.at[c, x + 2, pl.ds(yl, 2)], tiles.at[c, x + 2, pl.ds(0, 2)],
            ys_sem.at[0, c, x], yr_sem.at[0, c, x], up,
        )

    def y_down(c, x):
        return remote(
            tiles.at[c, x + 2, pl.ds(2, 2)], tiles.at[c, x + 2, pl.ds(yl + 2, 2)],
            ys_sem.at[1, c, x], yr_sem.at[1, c, x], down,
        )

    has_right, has_left = sx < nx - 1, sx > 0
    has_up, has_down = cr < nc - 1, cr > 0

    @pl.loop(0, 2)
    def _(r):
        @pl.loop(0, comps)
        def _(c):
            turn(r * comps + c)

            @pl.when(jnp.logical_and(has_right, c < last))
            def _():
                x_right(c, r).start()

            turn((r + 2) * comps + c)

            @pl.when(jnp.logical_and(has_left, c < last))
            def _():
                x_left(c, r).start()

    @pl.loop(0, yl)
    def _(y):
        @pl.when(has_right)
        def _():
            x_right_last(y).start()

        @pl.when(has_left)
        def _():
            x_left_last(y).start()

    def send_y(c, x):
        @pl.when(has_up)
        def _():
            y_up(c, x).start()

        @pl.when(has_down)
        def _():
            y_down(c, x).start()

    @pl.loop(4 * comps, xl * comps)
    def _(b):
        turn(b)
        send_y(b % comps, b // comps - 2)

    @pl.loop(0, 4 * comps)
    def _(b):
        send_y(b % comps, (b // comps + xl - 2) % xl)

    acc[...] = jnp.zeros_like(acc)
    step = 32

    def unit(x, y):
        px, py = x + 2, y + 2
        scale_x = mx[x] * F32(1.0 / 12.0)
        scale_y = my[y] * F32(1.0 / 12.0)
        for c in range(comps):
            dz[c] = jnp.dot(tiles[c, px, py], sz[...], preferred_element_type=F32) * mz[...]
        for s in range(0, snaps, step):
            part_rows = slice(s, s + step)

            def at(c, i, j):
                return tiles[c, px + i, py + j, part_rows].astype(F32)

            def along_x(c):
                return (8.0 * (at(c, 1, 0) - at(c, -1, 0)) - (at(c, 2, 0) - at(c, -2, 0))) * scale_x

            def along_y(c):
                return (8.0 * (at(c, 0, 1) - at(c, 0, -1)) - (at(c, 0, 2) - at(c, 0, -2))) * scale_y

            stack[x, y, 0, part_rows] = (along_y(2) - dz[1, part_rows]).astype(BF16)
            stack[x, y, 1, part_rows] = (dz[0, part_rows] - along_x(2)).astype(BF16)
            stack[x, y, 2, part_rows] = (along_x(1) - along_y(0)).astype(BF16)
            stack[x, y, 3, part_rows] = (along_x(0) + along_y(1) + dz[2, part_rows]).astype(BF16)
        both = (((1,), (1,)), ((), ()))
        total = acc[...]
        for f in range(4):
            cells = stack[x, y, f]
            total += lax.dot_general(cells, cells, both, preferred_element_type=F32)
        acc[...] = total

    def put(x):
        return pltpu.make_async_copy(stack.at[x], x_out.at[x], out_sem.at[x])

    def wait_y(x):
        for c in range(comps):
            @pl.when(has_down)
            def _():
                y_up(c, x).wait_recv()

            @pl.when(has_up)
            def _():
                y_down(c, x).wait_recv()

    @pl.loop(2, xl - 2)
    def _(x):
        wait_y(x)

        @pl.loop(0, yl)
        def _(y):
            unit(x, y)

        put(x).start()

    @pl.loop(0, 4)
    def _(i):
        wait_y((i + xl - 2) % xl)

    for c in range(last):
        for r in range(2):
            @pl.when(has_left)
            def _():
                x_right(c, r).wait_recv()

            @pl.when(has_right)
            def _():
                x_left(c, r).wait_recv()

    @pl.loop(0, yl)
    def _(y):
        @pl.when(has_left)
        def _():
            x_right_last(y).wait_recv()

        @pl.when(has_right)
        def _():
            x_left_last(y).wait_recv()

        @pl.loop(0, 4)
        def _(i):
            unit((i + xl - 2) % xl, y)

    @pl.loop(0, 4)
    def _(i):
        put((i + xl - 2) % xl).start()

    mine = pl.ds(pl.multiple_of(core * rows, rows), rows)
    other = pl.ds(pl.multiple_of((1 - core) * rows, rows), rows)
    swap = remote(acc.at[other], half, cs_sem, cr_sem, twin)
    swap.start()
    swap.wait()
    value = acc[mine, :] + half[...]
    stages = ((sx, nx, x_peer), (iy, ny, y_peer), (iz, nz, z_peer))
    for a, (me, count, peer) in enumerate(stages):
        part[a, me] = value
        copies = [
            remote(part.at[a, me], part.at[a, me], as_sem.at[a, k - 1], ar_sem.at[a, k - 1], peer(k))
            for k in range(1, count)
        ]
        for copy in copies:
            copy.start()
        for k in range(1, count):
            source = (me + count - k) % count
            remote(
                part.at[a, me], part.at[a, source], as_sem.at[a, k - 1], ar_sem.at[a, k - 1], peer(k)
            ).wait_recv()
        value = part[a, 0]
        for k in range(1, count):
            value = value + part[a, k]
        for copy in copies:
            copy.wait_send()
    whole[mine, :] = value
    final = remote(whole.at[mine], whole.at[mine], fs_sem, fr_sem, twin)
    final.start()
    final.wait_send()
    remote(whole.at[mine], whole.at[other], fs_sem, fr_sem, twin).wait_recv()
    gram_out[...] = whole[...]

    @pl.loop(0, xl)
    def _(x):
        put(x).wait()

    @pl.loop(0, comps * xl)
    def _(b):
        c, x = b % comps, b // comps

        @pl.when(has_up)
        def _():
            y_up(c, x).wait_send()

        @pl.when(has_down)
        def _():
            y_down(c, x).wait_send()

    for c in range(last):
        for r in range(2):
            @pl.when(has_right)
            def _():
                x_right(c, r).wait_send()

            @pl.when(has_left)
            def _():
                x_left(c, r).wait_send()

    @pl.loop(0, yl)
    def _(y):
        @pl.when(has_right)
        def _():
            x_right_last(y).wait_send()

        @pl.when(has_left)
        def _():
            x_left_last(y).wait_send()


def factorise(gram, work, upper, inverse):
    count = gram.shape[0]
    work[...] = gram
    lane = lax.broadcasted_iota(jnp.int32, (PANEL, count), 1)
    sub = lax.broadcasted_iota(jnp.int32, (PANEL, count), 0)
    for k0 in range(0, count, PANEL):
        rows = slice(k0, k0 + PANEL)
        block = work[rows, :]
        cols = [jnp.broadcast_to(block[:, k0 + j : k0 + j + 1], (PANEL, count)) for j in range(PANEL)]
        pivots = jnp.zeros((PANEL, count), F32)
        for j in range(PANEL):
            pivot = jnp.broadcast_to(cols[j][j : j + 1, :], (PANEL, count))
            row = jnp.broadcast_to(block[j : j + 1, :], (PANEL, count))
            pivots = jnp.where(sub == j, pivot, pivots)
            times = jnp.where(sub > j, cols[j] / pivot, 0.0)
            for i in range(j + 1, PANEL):
                cols[i] = cols[i] - times * jnp.broadcast_to(cols[i][j : j + 1, :], (PANEL, count))
            block = jnp.where(
                jnp.logical_and(lane == k0 + j, sub > j), -times, block - times * row
            )
        root = lax.rsqrt(pivots)
        upper[rows, :] = jnp.where(lane >= k0 + sub, block * root, 0.0)
        in_panel = jnp.logical_and(lane >= k0, lane < k0 + PANEL)
        left = jnp.where(
            lane == k0 + sub, 1.0, jnp.where(jnp.logical_and(in_panel, lane > k0 + sub), 0.0, block)
        )
        inverse[rows, :] = jnp.where(lane <= k0 + sub, left * root, 0.0).astype(inverse.dtype)
        if k0 + PANEL < count:
            below = slice(k0 + PANEL, count)
            times = jnp.where(lane >= k0 + PANEL, block / pivots, 0.0)
            change = lax.dot_general(
                times, left, (((0,), (0,)), ((), ())),
                preferred_element_type=F32, precision=lax.Precision.HIGHEST,
            )
            wide_lane = lax.broadcasted_iota(jnp.int32, (count - k0 - PANEL, count), 1)
            kept = jnp.where(
                jnp.logical_and(wide_lane >= k0, wide_lane < k0 + PANEL), 0.0, work[below, :]
            )
            work[below, :] = kept - change[k0 + PANEL :, :]


def modes_kernel(scale, gram, x, modes, factor, work, upper, inverse, wide):
    snaps, fields, _, yl, cz = modes.shape

    @pl.when(pl.program_id(0) == 0)
    def _():
        factorise(gram[...] * F32(scale), work, upper, inverse)
        factor[...] = upper[...].T

    for f in range(fields):
        for y in range(yl):
            wide[pl.ds(y, snaps, stride=yl), :] = jnp.dot(
                inverse[...], x[0, y, f], preferred_element_type=F32
            )
        modes[:, f, 0] = wide[...].reshape(snaps, yl, cz).astype(BF16)


def shards(sizes, velocity, metric_x, metric_y, metric_z):
    snaps, comps, xl, yl, cz = velocity.shape
    nx, ny, nz = sizes
    lanes = jnp.arange(cz)
    apart = lanes[:, None] - lanes[None, :]
    sz = (
        8.0 * (apart == 1) - 8.0 * (apart == -1) - 1.0 * (apart == 2) + 1.0 * (apart == -2)
    ).astype(BF16)
    mz = (metric_z * (1.0 / 12.0)).reshape(1, cz)
    rows = snaps // 2
    dma = pltpu.SemaphoreType.DMA
    most = max(sizes)
    stack, gram = pl.pallas_call(
        functools.partial(gram_kernel, sizes),
        out_shape=(
            jax.ShapeDtypeStruct((xl, yl, 4, snaps, cz), BF16),
            jax.ShapeDtypeStruct((snaps, snaps), F32),
        ),
        in_specs=[
            pl.BlockSpec(memory_space=pl.ANY),
            pl.BlockSpec(memory_space=pltpu.SMEM),
            pl.BlockSpec(memory_space=pltpu.SMEM),
            pl.BlockSpec(memory_space=pltpu.VMEM),
            pl.BlockSpec(memory_space=pltpu.VMEM),
        ],
        out_specs=(pl.BlockSpec(memory_space=pl.ANY), pl.BlockSpec(memory_space=pltpu.VMEM)),
        scratch_shapes=[
            pltpu.VMEM((comps * xl, snaps, yl, cz), BF16),
            pltpu.VMEM((comps, xl + 4, yl + 4, snaps, cz), BF16),
            pltpu.VMEM((xl, yl, 4, snaps, cz), BF16),
            pltpu.VMEM((snaps * yl, cz), F32),
            pltpu.VMEM((comps, snaps, cz), F32),
            pltpu.VMEM((snaps, snaps), F32),
            pltpu.VMEM((rows, snaps), F32),
            pltpu.VMEM((3, most, rows, snaps), F32),
            pltpu.VMEM((snaps, snaps), F32),
            dma((comps * xl,)),
            dma((xl,)),
            dma((2, comps - 1, 2)),
            dma((2, comps - 1, 2)),
            dma((2, yl)),
            dma((2, yl)),
            dma((2, comps, xl)),
            dma((2, comps, xl)),
            dma,
            dma,
            dma((3, most)),
            dma((3, most)),
            dma,
            dma,
        ],
        compiler_params=pltpu.CompilerParams(
            collective_id=0, has_side_effects=True, vmem_limit_bytes=VMEM_LIMIT
        ),
        name="fields_gram",
    )(velocity, metric_x, metric_y, mz, sz)
    scale = 1.0 / (4.0 * xl * nx * yl * ny * nz * 2 * cz)
    return pl.pallas_call(
        functools.partial(modes_kernel, scale),
        grid=(xl,),
        out_shape=(
            jax.ShapeDtypeStruct((snaps, 4, xl, yl, cz), BF16),
            jax.ShapeDtypeStruct((snaps, snaps), F32),
        ),
        in_specs=[
            pl.BlockSpec((snaps, snaps), lambda i: (0, 0)),
            pl.BlockSpec((1, yl, 4, snaps, cz), lambda i: (i, 0, 0, 0, 0)),
        ],
        out_specs=(
            pl.BlockSpec((snaps, 4, 1, yl, cz), lambda i: (0, 0, i, 0, 0)),
            pl.BlockSpec((snaps, snaps), lambda i: (0, 0)),
        ),
        scratch_shapes=[
            pltpu.VMEM((snaps, snaps), F32),
            pltpu.VMEM((snaps, snaps), F32),
            pltpu.VMEM((snaps, snaps), BF16),
            pltpu.VMEM((snaps * yl, cz), F32),
        ],
        compiler_params=pltpu.CompilerParams(
            dimension_semantics=("arbitrary",), vmem_limit_bytes=VMEM_LIMIT
        ),
        name="factor_modes",
    )(gram, stack)


def solution(mesh):
    across = mesh.shape["cross"]
    nz = 4 if across >= 32 else 2
    sizes = (mesh.shape["stream"], across // (2 * nz), nz)
    return jax.shard_map(
        functools.partial(shards, sizes),
        mesh=mesh,
        in_specs=(P(None, None, "stream", "cross", None), P("stream"), P("cross"), P()),
        out_specs=(P(None, None, "stream", "cross", None), P()),
        check_vma=False,
    )
```

```python
import functools

import jax
import jax.numpy as jnp
from jax import lax
from jax.experimental import pallas as pl
from jax.experimental.pallas import tpu as pltpu
from jax.sharding import PartitionSpec as P

MESH = pl.DeviceIdType.MESH
F32 = jnp.float32
BF16 = jnp.bfloat16
VMEM_LIMIT = 60 * 1024 * 1024
PANEL = 8


def gram_kernel(
    sizes, vel, mx, my, mz, sz, x_out, gram_out,
    raw, tiles, stack, wide, dz, acc, half, part, whole,
    load_sem, out_sem, xs_sem, xr_sem, xs2_sem, xr2_sem, ys_sem, yr_sem,
    cs_sem, cr_sem, as_sem, ar_sem, fs_sem, fr_sem,
):
    nx, ny, nz = sizes
    comps, xp, yp, snaps, cz = tiles.shape
    xl, yl = xp - 4, yp - 4
    nc = ny * nz * 2
    sx = lax.axis_index("stream")
    cr = lax.axis_index("cross")
    core = cr % 2
    iz = (cr // 2) % nz
    iy = cr // (2 * nz)
    rows = snaps // 2

    def x_peer(k):
        return ((sx + k) % nx, cr)

    def y_peer(k):
        return (sx, (((iy + k) % ny) * nz + iz) * 2 + core)

    def z_peer(k):
        return (sx, (iy * nz + (iz + k) % nz) * 2 + core)

    twin = (sx, cr + 1 - 2 * core)
    up = (sx, (cr + 1) % nc)
    down = (sx, (cr + nc - 1) % nc)

    def load(b):
        c, x = b % comps, (b // comps + xl - 2) % xl
        return pltpu.make_async_copy(vel.at[:, c, x], raw.at[b], load_sem.at[b])

    @pl.loop(0, comps * xl)
    def _(b):
        load(b).start()

    barrier = pltpu.get_barrier_semaphore()
    peers = [x_peer(k) for k in range(1, nx)] + [y_peer(k) for k in range(1, ny)]
    peers += [z_peer(k) for k in range(1, nz)] + [twin, up, down]
    for peer in peers:
        pl.semaphore_signal(barrier, inc=1, device_id=peer, device_id_type=MESH)

    @pl.when(sx == 0)
    def _():
        tiles[:, 0:2, 2 : yl + 2] = jnp.zeros((comps, 2, yl, snaps, cz), BF16)

    @pl.when(sx == nx - 1)
    def _():
        tiles[:, xl + 2 : xl + 4, 2 : yl + 2] = jnp.zeros((comps, 2, yl, snaps, cz), BF16)

    @pl.when(cr == 0)
    def _():
        tiles[:, 2 : xl + 2, 0:2] = jnp.zeros((comps, xl, 2, snaps, cz), BF16)

    @pl.when(cr == nc - 1)
    def _():
        tiles[:, 2 : xl + 2, yl + 2 : yl + 4] = jnp.zeros((comps, xl, 2, snaps, cz), BF16)

    pl.semaphore_wait(barrier, len(peers))

    def turn(b):
        c, x = b % comps, (b // comps + xl - 2) % xl
        load(b).wait()
        wide[...] = raw[b].astype(F32).reshape(snaps * yl, cz)
        for y in range(yl):
            tiles[c, x + 2, y + 2] = wide[pl.ds(y, snaps, stride=yl), :].astype(BF16)

    def remote(src, dst, send, recv, peer):
        return pltpu.make_async_remote_copy(
            src_ref=src, dst_ref=dst, send_sem=send, recv_sem=recv,
            device_id=peer, device_id_type=MESH,
        )

    right = ((sx + 1) % nx, cr)
    left = ((sx + nx - 1) % nx, cr)
    inner = pl.ds(2, yl)

    def x_right(c, r):
        return remote(
            tiles.at[c, xl + r, inner], tiles.at[c, r, inner],
            xs_sem.at[0, c, r], xr_sem.at[0, c, r], right,
        )

    def x_left(c, r):
        return remote(
            tiles.at[c, 2 + r, inner], tiles.at[c, xl + 2 + r, inner],
            xs_sem.at[1, c, r], xr_sem.at[1, c, r], left,
        )

    last = comps - 1

    def x_right_last(y):
        return remote(
            tiles.at[last, pl.ds(xl, 2), y + 2], tiles.at[last, pl.ds(0, 2), y + 2],
            xs2_sem.at[0, y], xr2_sem.at[0, y], right,
        )

    def x_left_last(y):
        return remote(
            tiles.at[last, pl.ds(2, 2), y + 2], tiles.at[last, pl.ds(xl + 2, 2), y + 2],
            xs2_sem.at[1, y], xr2_sem.at[1, y], left,
        )

    def y_up(c, x):
        return remote(
            tiles.at[c, x + 2, pl.ds(yl, 2)], tiles.at[c, x + 2, pl.ds(0, 2)],
            ys_sem.at[0, c, x], yr_sem.at[0, c, x], up,
        )

    def y_down(c, x):
        return remote(
            tiles.at[c, x + 2, pl.ds(2, 2)], tiles.at[c, x + 2, pl.ds(yl + 2, 2)],
            ys_sem.at[1, c, x], yr_sem.at[1, c, x], down,
        )

    has_right, has_left = sx < nx - 1, sx > 0
    has_up, has_down = cr < nc - 1, cr > 0

    @pl.loop(0, 2)
    def _(r):
        @pl.loop(0, comps)
        def _(c):
            turn(r * comps + c)

            @pl.when(jnp.logical_and(has_right, c < last))
            def _():
                x_right(c, r).start()

            turn((r + 2) * comps + c)

            @pl.when(jnp.logical_and(has_left, c < last))
            def _():
                x_left(c, r).start()

    @pl.loop(0, yl)
    def _(y):
        @pl.when(has_right)
        def _():
            x_right_last(y).start()

        @pl.when(has_left)
        def _():
            x_left_last(y).start()

    def send_y(c, x):
        @pl.when(has_up)
        def _():
            y_up(c, x).start()

        @pl.when(has_down)
        def _():
            y_down(c, x).start()

    @pl.loop(4 * comps, xl * comps)
    def _(b):
        turn(b)
        send_y(b % comps, b // comps - 2)

    @pl.loop(0, 4 * comps)
    def _(b):
        send_y(b % comps, (b // comps + xl - 2) % xl)

    acc[...] = jnp.zeros_like(acc)
    step = 32

    def fields(slot, x, y):
        px, py = x + 2, y + 2
        scale_x = mx[x] * F32(1.0 / 12.0)
        for s in range(0, snaps, step):
            part_rows = slice(s, s + step)
            scale_y = [my[y + k] * F32(1.0 / 12.0) for k in range(2)]

            def at(c, i, j):
                return tiles[c, px + i, py + j, part_rows].astype(F32)

            column = [[at(c, 0, j) for j in range(-2, 4)] for c in range(comps)]

            def along_x(c, k):
                return (8.0 * (at(c, 1, k) - at(c, -1, k)) - (at(c, 2, k) - at(c, -2, k))) * scale_x

            def along_y(c, k):
                f = column[c][k : k + 5]
                return (8.0 * (f[3] - f[1]) - (f[4] - f[0])) * scale_y[k]

            for k in range(2):
                along_z = [dz[slot, c, part_rows, k * cz : (k + 1) * cz] for c in range(comps)]
                stack[x, y + k, 0, part_rows] = (along_y(2, k) - along_z[1]).astype(BF16)
                stack[x, y + k, 1, part_rows] = (along_z[0] - along_x(2, k)).astype(BF16)
                stack[x, y + k, 2, part_rows] = (along_x(1, k) - along_y(0, k)).astype(BF16)
                stack[x, y + k, 3, part_rows] = (
                    along_x(0, k) + along_y(1, k) + along_z[2]
                ).astype(BF16)

    def products(x, y):
        both = (((1,), (1,)), ((), ()))
        total = acc[...]
        for k in range(2):
            for f in range(0, 4, 2):
                cells = jnp.concatenate([stack[x, y + k, f], stack[x, y + k, f + 1]], axis=1)
                total += lax.dot_general(cells, cells, both, preferred_element_type=F32)
        acc[...] = total

    def units(*cells):
        for slot, (x, y) in enumerate(cells):
            for c in range(comps):
                pair = jnp.concatenate([tiles[c, x + 2, y + 2], tiles[c, x + 2, y + 3]], axis=1)
                dz[slot, c] = jnp.dot(pair, sz[...], preferred_element_type=F32) * mz[...]
        for slot, (x, y) in enumerate(cells):
            fields(slot, x, y)
            products(x, y)

    def put(x):
        return pltpu.make_async_copy(stack.at[x], x_out.at[x], out_sem.at[x])

    def wait_y(x):
        for c in range(comps):
            @pl.when(has_down)
            def _():
                y_up(c, x).wait_recv()

            @pl.when(has_up)
            def _():
                y_down(c, x).wait_recv()

    @pl.loop(2, xl - 2)
    def _(x):
        wait_y(x)

        @pl.loop(0, yl // 4)
        def _(h):
            units((x, 4 * h), (x, 4 * h + 2))

        put(x).start()

    @pl.loop(0, 4)
    def _(i):
        wait_y((i + xl - 2) % xl)

    for c in range(last):
        for r in range(2):
            @pl.when(has_left)
            def _():
                x_right(c, r).wait_recv()

            @pl.when(has_right)
            def _():
                x_left(c, r).wait_recv()

    @pl.loop(0, yl // 2)
    def _(h):
        for k in range(2):
            @pl.when(has_left)
            def _():
                x_right_last(2 * h + k).wait_recv()

            @pl.when(has_right)
            def _():
                x_left_last(2 * h + k).wait_recv()

        @pl.loop(0, 2)
        def _(i):
            units(((2 * i + xl - 2) % xl, 2 * h), ((2 * i + xl - 1) % xl, 2 * h))

    @pl.loop(0, 4)
    def _(i):
        put((i + xl - 2) % xl).start()

    mine = pl.ds(pl.multiple_of(core * rows, rows), rows)
    other = pl.ds(pl.multiple_of((1 - core) * rows, rows), rows)
    swap = remote(acc.at[other], half, cs_sem, cr_sem, twin)
    swap.start()
    swap.wait()
    value = acc[mine, :] + half[...]
    stages = ((sx, nx, x_peer), (iy, ny, y_peer), (iz, nz, z_peer))
    for a, (me, count, peer) in enumerate(stages):
        part[a, me] = value
        copies = [
            remote(part.at[a, me], part.at[a, me], as_sem.at[a, k - 1], ar_sem.at[a, k - 1], peer(k))
            for k in range(1, count)
        ]
        for copy in copies:
            copy.start()
        for k in range(1, count):
            source = (me + count - k) % count
            remote(
                part.at[a, me], part.at[a, source], as_sem.at[a, k - 1], ar_sem.at[a, k - 1], peer(k)
            ).wait_recv()
        value = part[a, 0]
        for k in range(1, count):
            value = value + part[a, k]
        for copy in copies:
            copy.wait_send()
    whole[mine, :] = value
    final = remote(whole.at[mine], whole.at[mine], fs_sem, fr_sem, twin)
    final.start()
    final.wait_send()
    remote(whole.at[mine], whole.at[other], fs_sem, fr_sem, twin).wait_recv()
    gram_out[...] = whole[...]

    @pl.loop(0, xl)
    def _(x):
        put(x).wait()

    @pl.loop(0, comps * xl)
    def _(b):
        c, x = b % comps, b // comps

        @pl.when(has_up)
        def _():
            y_up(c, x).wait_send()

        @pl.when(has_down)
        def _():
            y_down(c, x).wait_send()

    for c in range(last):
        for r in range(2):
            @pl.when(has_right)
            def _():
                x_right(c, r).wait_send()

            @pl.when(has_left)
            def _():
                x_left(c, r).wait_send()

    @pl.loop(0, yl)
    def _(y):
        @pl.when(has_right)
        def _():
            x_right_last(y).wait_send()

        @pl.when(has_left)
        def _():
            x_left_last(y).wait_send()


def factorise(gram, work, upper, inverse):
    count = gram.shape[0]
    work[...] = gram
    lane = lax.broadcasted_iota(jnp.int32, (PANEL, count), 1)
    sub = lax.broadcasted_iota(jnp.int32, (PANEL, count), 0)
    for k0 in range(0, count, PANEL):
        rows = slice(k0, k0 + PANEL)
        block = work[rows, :]
        cols = [jnp.broadcast_to(block[:, k0 + j : k0 + j + 1], (PANEL, count)) for j in range(PANEL)]
        pivots = jnp.zeros((PANEL, count), F32)
        for j in range(PANEL):
            pivot = jnp.broadcast_to(cols[j][j : j + 1, :], (PANEL, count))
            row = jnp.broadcast_to(block[j : j + 1, :], (PANEL, count))
            pivots = jnp.where(sub == j, pivot, pivots)
            times = jnp.where(sub > j, cols[j] / pivot, 0.0)
            for i in range(j + 1, PANEL):
                cols[i] = cols[i] - times * jnp.broadcast_to(cols[i][j : j + 1, :], (PANEL, count))
            block = jnp.where(
                jnp.logical_and(lane == k0 + j, sub > j), -times, block - times * row
            )
        root = lax.rsqrt(pivots)
        upper[rows, :] = jnp.where(lane >= k0 + sub, block * root, 0.0)
        in_panel = jnp.logical_and(lane >= k0, lane < k0 + PANEL)
        left = jnp.where(
            lane == k0 + sub, 1.0, jnp.where(jnp.logical_and(in_panel, lane > k0 + sub), 0.0, block)
        )
        inverse[rows, :] = jnp.where(lane <= k0 + sub, left * root, 0.0).astype(inverse.dtype)
        if k0 + PANEL < count:
            below = slice(k0 + PANEL, count)
            times = jnp.where(lane >= k0 + PANEL, block / pivots, 0.0)
            change = lax.dot_general(
                times, left, (((0,), (0,)), ((), ())),
                preferred_element_type=F32, precision=lax.Precision.HIGHEST,
            )
            wide_lane = lax.broadcasted_iota(jnp.int32, (count - k0 - PANEL, count), 1)
            kept = jnp.where(
                jnp.logical_and(wide_lane >= k0, wide_lane < k0 + PANEL), 0.0, work[below, :]
            )
            work[below, :] = kept - change[k0 + PANEL :, :]


def modes_kernel(scale, gram, x, modes, factor, work, upper, inverse, wide):
    snaps, fields, _, yl, cz = modes.shape

    @pl.when(pl.program_id(0) == 0)
    def _():
        factorise(gram[...] * F32(scale), work, upper, inverse)
        factor[...] = upper[...].T

    for f in range(fields):
        for y in range(yl):
            wide[pl.ds(y, snaps, stride=yl), :] = jnp.dot(
                inverse[...], x[0, y, f], preferred_element_type=F32
            )
        modes[:, f, 0] = wide[...].reshape(snaps, yl, cz).astype(BF16)


def shards(sizes, velocity, metric_x, metric_y, metric_z):
    snaps, comps, xl, yl, cz = velocity.shape
    nx, ny, nz = sizes
    lanes = jnp.arange(2 * cz)
    apart = lanes[:, None] - lanes[None, :]
    same = lanes[:, None] // cz == lanes[None, :] // cz
    sz = same * (
        8.0 * (apart == 1) - 8.0 * (apart == -1) - 1.0 * (apart == 2) + 1.0 * (apart == -2)
    )
    sz = sz.astype(BF16)
    mz = jnp.tile((metric_z * (1.0 / 12.0)).reshape(1, cz), (1, 2))
    rows = snaps // 2
    dma = pltpu.SemaphoreType.DMA
    most = max(sizes)
    stack, gram = pl.pallas_call(
        functools.partial(gram_kernel, sizes),
        out_shape=(
            jax.ShapeDtypeStruct((xl, yl, 4, snaps, cz), BF16),
            jax.ShapeDtypeStruct((snaps, snaps), F32),
        ),
        in_specs=[
            pl.BlockSpec(memory_space=pl.ANY),
            pl.BlockSpec(memory_space=pltpu.SMEM),
            pl.BlockSpec(memory_space=pltpu.SMEM),
            pl.BlockSpec(memory_space=pltpu.VMEM),
            pl.BlockSpec(memory_space=pltpu.VMEM),
        ],
        out_specs=(pl.BlockSpec(memory_space=pl.ANY), pl.BlockSpec(memory_space=pltpu.VMEM)),
        scratch_shapes=[
            pltpu.VMEM((comps * xl, snaps, yl, cz), BF16),
            pltpu.VMEM((comps, xl + 4, yl + 4, snaps, cz), BF16),
            pltpu.VMEM((xl, yl, 4, snaps, cz), BF16),
            pltpu.VMEM((snaps * yl, cz), F32),
            pltpu.VMEM((2, comps, snaps, 2 * cz), F32),
            pltpu.VMEM((snaps, snaps), F32),
            pltpu.VMEM((rows, snaps), F32),
            pltpu.VMEM((3, most, rows, snaps), F32),
            pltpu.VMEM((snaps, snaps), F32),
            dma((comps * xl,)),
            dma((xl,)),
            dma((2, comps - 1, 2)),
            dma((2, comps - 1, 2)),
            dma((2, yl)),
            dma((2, yl)),
            dma((2, comps, xl)),
            dma((2, comps, xl)),
            dma,
            dma,
            dma((3, most)),
            dma((3, most)),
            dma,
            dma,
        ],
        compiler_params=pltpu.CompilerParams(
            collective_id=0, has_side_effects=True, vmem_limit_bytes=VMEM_LIMIT
        ),
        name="fields_gram",
    )(velocity, metric_x, metric_y, mz, sz)
    scale = 1.0 / (4.0 * xl * nx * yl * ny * nz * 2 * cz)
    return pl.pallas_call(
        functools.partial(modes_kernel, scale),
        grid=(xl,),
        out_shape=(
            jax.ShapeDtypeStruct((snaps, 4, xl, yl, cz), BF16),
            jax.ShapeDtypeStruct((snaps, snaps), F32),
        ),
        in_specs=[
            pl.BlockSpec((snaps, snaps), lambda i: (0, 0)),
            pl.BlockSpec((1, yl, 4, snaps, cz), lambda i: (i, 0, 0, 0, 0)),
        ],
        out_specs=(
            pl.BlockSpec((snaps, 4, 1, yl, cz), lambda i: (0, 0, i, 0, 0)),
            pl.BlockSpec((snaps, snaps), lambda i: (0, 0)),
        ),
        scratch_shapes=[
            pltpu.VMEM((snaps, snaps), F32),
            pltpu.VMEM((snaps, snaps), F32),
            pltpu.VMEM((snaps, snaps), BF16),
            pltpu.VMEM((snaps * yl, cz), F32),
        ],
        compiler_params=pltpu.CompilerParams(
            dimension_semantics=("arbitrary",), vmem_limit_bytes=VMEM_LIMIT
        ),
        name="factor_modes",
    )(gram, stack)


def solution(mesh):
    across = mesh.shape["cross"]
    nz = 4 if across >= 32 else 2
    sizes = (mesh.shape["stream"], across // (2 * nz), nz)
    return jax.shard_map(
        functools.partial(shards, sizes),
        mesh=mesh,
        in_specs=(P(None, None, "stream", "cross", None), P("stream"), P("cross"), P()),
        out_specs=(P(None, None, "stream", "cross", None), P()),
        check_vma=False,
    )
```

```python
import functools

import jax
import jax.numpy as jnp
import numpy as np
from jax import lax
from jax.experimental import pallas as pl
from jax.experimental.pallas import tpu as pltpu
from jax.sharding import PartitionSpec as P

MESH = pl.DeviceIdType.MESH
F32 = jnp.float32
BF16 = jnp.bfloat16
VMEM_LIMIT = 60 * 1024 * 1024
PANEL = 8


def gram_kernel(
    sizes, vel, mx, my, mz, sz, x_out, gram_out,
    raw, tiles, stack, wide, scale_z, dz, acc, half, part, whole,
    load_sem, out_sem, xs_sem, xr_sem, xs2_sem, xr2_sem, ys_sem, yr_sem,
    cs_sem, cr_sem, as_sem, ar_sem, fs_sem, fr_sem,
):
    nx, ny, nz = sizes
    comps, xp, yp, snaps, cz = tiles.shape
    xl, yl = xp - 4, yp - 4
    nc = ny * nz * 2
    sx = lax.axis_index("stream")
    cr = lax.axis_index("cross")
    core = cr % 2
    iz = (cr // 2) % nz
    iy = cr // (2 * nz)
    rows = snaps // 2

    def x_peer(k):
        return ((sx + k) % nx, cr)

    def y_peer(k):
        return (sx, (((iy + k) % ny) * nz + iz) * 2 + core)

    def z_peer(k):
        return (sx, (iy * nz + (iz + k) % nz) * 2 + core)

    twin = (sx, cr + 1 - 2 * core)
    up = (sx, (cr + 1) % nc)
    down = (sx, (cr + nc - 1) % nc)

    def load(b):
        c, x = b % comps, (b // comps + xl - 2) % xl
        return pltpu.make_async_copy(vel.at[:, c, x], raw.at[b], load_sem.at[b])

    @pl.loop(0, comps * xl)
    def _(b):
        load(b).start()

    barrier = pltpu.get_barrier_semaphore()
    peers = [x_peer(k) for k in range(1, nx)] + [y_peer(k) for k in range(1, ny)]
    peers += [z_peer(k) for k in range(1, nz)] + [twin, up, down]
    for peer in peers:
        pl.semaphore_signal(barrier, inc=1, device_id=peer, device_id_type=MESH)

    @pl.when(sx == 0)
    def _():
        tiles[:, 0:2, 2 : yl + 2] = jnp.zeros((comps, 2, yl, snaps, cz), BF16)

    @pl.when(sx == nx - 1)
    def _():
        tiles[:, xl + 2 : xl + 4, 2 : yl + 2] = jnp.zeros((comps, 2, yl, snaps, cz), BF16)

    @pl.when(cr == 0)
    def _():
        tiles[:, 2 : xl + 2, 0:2] = jnp.zeros((comps, xl, 2, snaps, cz), BF16)

    @pl.when(cr == nc - 1)
    def _():
        tiles[:, 2 : xl + 2, yl + 2 : yl + 4] = jnp.zeros((comps, xl, 2, snaps, cz), BF16)

    pl.semaphore_wait(barrier, len(peers))

    def turn(b):
        c, x = b % comps, (b // comps + xl - 2) % xl
        load(b).wait()
        wide[...] = raw[b].astype(F32).reshape(snaps * yl, cz)
        for y in range(yl):
            tiles[c, x + 2, y + 2] = wide[pl.ds(y, snaps, stride=yl), :].astype(BF16)

    def remote(src, dst, send, recv, peer):
        return pltpu.make_async_remote_copy(
            src_ref=src, dst_ref=dst, send_sem=send, recv_sem=recv,
            device_id=peer, device_id_type=MESH,
        )

    right = ((sx + 1) % nx, cr)
    left = ((sx + nx - 1) % nx, cr)
    inner = pl.ds(2, yl)

    def x_right(c, r):
        return remote(
            tiles.at[c, xl + r, inner], tiles.at[c, r, inner],
            xs_sem.at[0, c, r], xr_sem.at[0, c, r], right,
        )

    def x_left(c, r):
        return remote(
            tiles.at[c, 2 + r, inner], tiles.at[c, xl + 2 + r, inner],
            xs_sem.at[1, c, r], xr_sem.at[1, c, r], left,
        )

    last = comps - 1

    def x_right_last(y):
        return remote(
            tiles.at[last, pl.ds(xl, 2), y + 2], tiles.at[last, pl.ds(0, 2), y + 2],
            xs2_sem.at[0, y], xr2_sem.at[0, y], right,
        )

    def x_left_last(y):
        return remote(
            tiles.at[last, pl.ds(2, 2), y + 2], tiles.at[last, pl.ds(xl + 2, 2), y + 2],
            xs2_sem.at[1, y], xr2_sem.at[1, y], left,
        )

    def y_up(c, x):
        return remote(
            tiles.at[c, x + 2, pl.ds(yl, 2)], tiles.at[c, x + 2, pl.ds(0, 2)],
            ys_sem.at[0, c, x], yr_sem.at[0, c, x], up,
        )

    def y_down(c, x):
        return remote(
            tiles.at[c, x + 2, pl.ds(2, 2)], tiles.at[c, x + 2, pl.ds(yl + 2, 2)],
            ys_sem.at[1, c, x], yr_sem.at[1, c, x], down,
        )

    has_right, has_left = sx < nx - 1, sx > 0
    has_up, has_down = cr < nc - 1, cr > 0

    @pl.loop(0, 2)
    def _(r):
        @pl.loop(0, comps)
        def _(c):
            turn(r * comps + c)

            @pl.when(jnp.logical_and(has_right, c < last))
            def _():
                x_right(c, r).start()

            turn((r + 2) * comps + c)

            @pl.when(jnp.logical_and(has_left, c < last))
            def _():
                x_left(c, r).start()

    @pl.loop(0, yl)
    def _(y):
        @pl.when(has_right)
        def _():
            x_right_last(y).start()

        @pl.when(has_left)
        def _():
            x_left_last(y).start()

    def send_y(c, x):
        @pl.when(has_up)
        def _():
            y_up(c, x).start()

        @pl.when(has_down)
        def _():
            y_down(c, x).start()

    @pl.loop(4 * comps, xl * comps)
    def _(b):
        turn(b)
        send_y(b % comps, b // comps - 2)

    @pl.loop(0, 4 * comps)
    def _(b):
        send_y(b % comps, (b // comps + xl - 2) % xl)

    acc[...] = jnp.zeros_like(acc)
    scale_z[:, :cz] = mz[...] * F32(1.0 / 12.0)
    scale_z[:, cz:] = mz[...] * F32(1.0 / 12.0)
    step = 32

    def fields(slot, x, y):
        px, py = x + 2, y + 2
        scale_x = mx[x] * F32(1.0 / 12.0)
        for s in range(0, snaps, step):
            part_rows = slice(s, s + step)
            scale_y = [my[y + k] * F32(1.0 / 12.0) for k in range(2)]

            def at(c, i, j):
                return tiles[c, px + i, py + j, part_rows].astype(F32)

            column = [[at(c, 0, j) for j in range(-2, 4)] for c in range(comps)]

            def along_x(c, k):
                return (8.0 * (at(c, 1, k) - at(c, -1, k)) - (at(c, 2, k) - at(c, -2, k))) * scale_x

            def along_y(c, k):
                f = column[c][k : k + 5]
                return (8.0 * (f[3] - f[1]) - (f[4] - f[0])) * scale_y[k]

            for k in range(2):
                along_z = [dz[slot, c, part_rows, k * cz : (k + 1) * cz] for c in range(comps)]
                stack[x, y + k, 0, part_rows] = (along_y(2, k) - along_z[1]).astype(BF16)
                stack[x, y + k, 1, part_rows] = (along_z[0] - along_x(2, k)).astype(BF16)
                stack[x, y + k, 2, part_rows] = (along_x(1, k) - along_y(0, k)).astype(BF16)
                stack[x, y + k, 3, part_rows] = (
                    along_x(0, k) + along_y(1, k) + along_z[2]
                ).astype(BF16)

    def products(x, y):
        both = (((1,), (1,)), ((), ()))
        total = acc[...]
        for k in range(2):
            for f in range(0, 4, 2):
                cells = jnp.concatenate([stack[x, y + k, f], stack[x, y + k, f + 1]], axis=1)
                total += lax.dot_general(cells, cells, both, preferred_element_type=F32)
        acc[...] = total

    def units(*cells):
        for slot, (x, y) in enumerate(cells):
            for c in range(comps):
                pair = jnp.concatenate([tiles[c, x + 2, y + 2], tiles[c, x + 2, y + 3]], axis=1)
                dz[slot, c] = jnp.dot(pair, sz[...], preferred_element_type=F32) * scale_z[...]
        for slot, (x, y) in enumerate(cells):
            fields(slot, x, y)
            products(x, y)

    def put(x):
        return pltpu.make_async_copy(stack.at[x], x_out.at[x], out_sem.at[x])

    def wait_y(x):
        for c in range(comps):
            @pl.when(has_down)
            def _():
                y_up(c, x).wait_recv()

            @pl.when(has_up)
            def _():
                y_down(c, x).wait_recv()

    @pl.loop(2, xl - 2)
    def _(x):
        wait_y(x)

        @pl.loop(0, yl // 4)
        def _(h):
            units((x, 4 * h), (x, 4 * h + 2))

        put(x).start()

    @pl.loop(0, 4)
    def _(i):
        wait_y((i + xl - 2) % xl)

    for c in range(last):
        for r in range(2):
            @pl.when(has_left)
            def _():
                x_right(c, r).wait_recv()

            @pl.when(has_right)
            def _():
                x_left(c, r).wait_recv()

    @pl.loop(0, yl // 2)
    def _(h):
        for k in range(2):
            @pl.when(has_left)
            def _():
                x_right_last(2 * h + k).wait_recv()

            @pl.when(has_right)
            def _():
                x_left_last(2 * h + k).wait_recv()

        @pl.loop(0, 2)
        def _(i):
            units(((2 * i + xl - 2) % xl, 2 * h), ((2 * i + xl - 1) % xl, 2 * h))

    @pl.loop(0, 4)
    def _(i):
        put((i + xl - 2) % xl).start()

    mine = pl.ds(pl.multiple_of(core * rows, rows), rows)
    other = pl.ds(pl.multiple_of((1 - core) * rows, rows), rows)
    swap = remote(acc.at[other], half, cs_sem, cr_sem, twin)
    swap.start()
    swap.wait()
    value = acc[mine, :] + half[...]
    stages = ((sx, nx, x_peer), (iy, ny, y_peer), (iz, nz, z_peer))
    for a, (me, count, peer) in enumerate(stages):
        part[a, me] = value
        copies = [
            remote(part.at[a, me], part.at[a, me], as_sem.at[a, k - 1], ar_sem.at[a, k - 1], peer(k))
            for k in range(1, count)
        ]
        for copy in copies:
            copy.start()
        for k in range(1, count):
            source = (me + count - k) % count
            remote(
                part.at[a, me], part.at[a, source], as_sem.at[a, k - 1], ar_sem.at[a, k - 1], peer(k)
            ).wait_recv()
        value = part[a, 0]
        for k in range(1, count):
            value = value + part[a, k]
        for copy in copies:
            copy.wait_send()
    whole[mine, :] = value
    final = remote(whole.at[mine], whole.at[mine], fs_sem, fr_sem, twin)
    final.start()
    final.wait_send()
    remote(whole.at[mine], whole.at[other], fs_sem, fr_sem, twin).wait_recv()
    gram_out[...] = whole[...]

    @pl.loop(0, xl)
    def _(x):
        put(x).wait()

    @pl.loop(0, comps * xl)
    def _(b):
        c, x = b % comps, b // comps

        @pl.when(has_up)
        def _():
            y_up(c, x).wait_send()

        @pl.when(has_down)
        def _():
            y_down(c, x).wait_send()

    for c in range(last):
        for r in range(2):
            @pl.when(has_right)
            def _():
                x_right(c, r).wait_send()

            @pl.when(has_left)
            def _():
                x_left(c, r).wait_send()

    @pl.loop(0, yl)
    def _(y):
        @pl.when(has_right)
        def _():
            x_right_last(y).wait_send()

        @pl.when(has_left)
        def _():
            x_left_last(y).wait_send()


def factorise(gram, work, upper, inverse):
    count = gram.shape[0]
    work[...] = gram
    lane = lax.broadcasted_iota(jnp.int32, (PANEL, count), 1)
    sub = lax.broadcasted_iota(jnp.int32, (PANEL, count), 0)
    for k0 in range(0, count, PANEL):
        rows = slice(k0, k0 + PANEL)
        block = work[rows, :]
        cols = [jnp.broadcast_to(block[:, k0 + j : k0 + j + 1], (PANEL, count)) for j in range(PANEL)]
        pivots = jnp.zeros((PANEL, count), F32)
        for j in range(PANEL):
            pivot = jnp.broadcast_to(cols[j][j : j + 1, :], (PANEL, count))
            row = jnp.broadcast_to(block[j : j + 1, :], (PANEL, count))
            pivots = jnp.where(sub == j, pivot, pivots)
            times = jnp.where(sub > j, cols[j] / pivot, 0.0)
            for i in range(j + 1, PANEL):
                cols[i] = cols[i] - times * jnp.broadcast_to(cols[i][j : j + 1, :], (PANEL, count))
            block = jnp.where(
                jnp.logical_and(lane == k0 + j, sub > j), -times, block - times * row
            )
        root = lax.rsqrt(pivots)
        upper[rows, :] = jnp.where(lane >= k0 + sub, block * root, 0.0)
        in_panel = jnp.logical_and(lane >= k0, lane < k0 + PANEL)
        left = jnp.where(
            lane == k0 + sub, 1.0, jnp.where(jnp.logical_and(in_panel, lane > k0 + sub), 0.0, block)
        )
        inverse[rows, :] = jnp.where(lane <= k0 + sub, left * root, 0.0).astype(inverse.dtype)
        if k0 + PANEL < count:
            below = slice(k0 + PANEL, count)
            times = jnp.where(lane >= k0 + PANEL, block / pivots, 0.0)
            change = lax.dot_general(
                times, left, (((0,), (0,)), ((), ())),
                preferred_element_type=F32, precision=lax.Precision.HIGHEST,
            )
            wide_lane = lax.broadcasted_iota(jnp.int32, (count - k0 - PANEL, count), 1)
            kept = jnp.where(
                jnp.logical_and(wide_lane >= k0, wide_lane < k0 + PANEL), 0.0, work[below, :]
            )
            work[below, :] = kept - change[k0 + PANEL :, :]


def modes_kernel(scale, gram, x, modes, factor, work, upper, inverse, held, sem):
    fields, yl = modes.shape[1], modes.shape[3]
    cz = modes.shape[4]
    step = pl.program_id(0)

    def fetch(i):
        return pltpu.make_async_copy(x.at[i], held.at[i], sem.at[i])

    @pl.when(step == 0)
    def _():
        for i in range(x.shape[0]):
            fetch(i).start()
        factorise(gram[...] * F32(scale), work, upper, inverse)
        factor[...] = upper[...].T

    fetch(step).wait()
    for f in range(fields):
        rows = []
        for y in range(0, yl, 2):
            pair = jnp.concatenate([held[step, y, f], held[step, y + 1, f]], axis=1)
            both = jnp.dot(inverse[...], pair, preferred_element_type=F32).astype(BF16)
            rows += [both[:, :cz], both[:, cz:]]
        modes[:, f, 0] = jnp.swapaxes(jnp.stack(rows, axis=0), 0, 1)


def shards(sizes, velocity, metric_x, metric_y, metric_z):
    snaps, comps, xl, yl, cz = velocity.shape
    nx, ny, nz = sizes
    lanes = np.arange(2 * cz)
    apart = lanes[:, None] - lanes[None, :]
    same = lanes[:, None] // cz == lanes[None, :] // cz
    stencil = 8.0 * (apart == 1) - 8.0 * (apart == -1) - 1.0 * (apart == 2) + 1.0 * (apart == -2)
    sz = jnp.asarray(same * stencil, BF16)
    mz = metric_z.reshape(1, cz)
    rows = snaps // 2
    dma = pltpu.SemaphoreType.DMA
    most = max(sizes)
    stack, gram = pl.pallas_call(
        functools.partial(gram_kernel, sizes),
        out_shape=(
            jax.ShapeDtypeStruct((xl, yl, 4, snaps, cz), BF16),
            jax.ShapeDtypeStruct((snaps, snaps), F32),
        ),
        in_specs=[
            pl.BlockSpec(memory_space=pl.ANY),
            pl.BlockSpec(memory_space=pltpu.SMEM),
            pl.BlockSpec(memory_space=pltpu.SMEM),
            pl.BlockSpec(memory_space=pltpu.VMEM),
            pl.BlockSpec(memory_space=pltpu.VMEM),
        ],
        out_specs=(pl.BlockSpec(memory_space=pl.ANY), pl.BlockSpec(memory_space=pltpu.VMEM)),
        scratch_shapes=[
            pltpu.VMEM((comps * xl, snaps, yl, cz), BF16),
            pltpu.VMEM((comps, xl + 4, yl + 4, snaps, cz), BF16),
            pltpu.VMEM((xl, yl, 4, snaps, cz), BF16),
            pltpu.VMEM((snaps * yl, cz), F32),
            pltpu.VMEM((1, 2 * cz), F32),
            pltpu.VMEM((2, comps, snaps, 2 * cz), F32),
            pltpu.VMEM((snaps, snaps), F32),
            pltpu.VMEM((rows, snaps), F32),
            pltpu.VMEM((3, most, rows, snaps), F32),
            pltpu.VMEM((snaps, snaps), F32),
            dma((comps * xl,)),
            dma((xl,)),
            dma((2, comps - 1, 2)),
            dma((2, comps - 1, 2)),
            dma((2, yl)),
            dma((2, yl)),
            dma((2, comps, xl)),
            dma((2, comps, xl)),
            dma,
            dma,
            dma((3, most)),
            dma((3, most)),
            dma,
            dma,
        ],
        compiler_params=pltpu.CompilerParams(
            collective_id=0, has_side_effects=True, vmem_limit_bytes=VMEM_LIMIT
        ),
        name="fields_gram",
    )(velocity, metric_x, metric_y, mz, sz)
    scale = 1.0 / (4.0 * xl * nx * yl * ny * nz * 2 * cz)
    return pl.pallas_call(
        functools.partial(modes_kernel, scale),
        grid=(xl,),
        out_shape=(
            jax.ShapeDtypeStruct((snaps, 4, xl, yl, cz), BF16),
            jax.ShapeDtypeStruct((snaps, snaps), F32),
        ),
        in_specs=[
            pl.BlockSpec((snaps, snaps), lambda i: (0, 0)),
            pl.BlockSpec(memory_space=pl.ANY),
        ],
        out_specs=(
            pl.BlockSpec((snaps, 4, 1, yl, cz), lambda i: (0, 0, i, 0, 0)),
            pl.BlockSpec((snaps, snaps), lambda i: (0, 0)),
        ),
        scratch_shapes=[
            pltpu.VMEM((snaps, snaps), F32),
            pltpu.VMEM((snaps, snaps), F32),
            pltpu.VMEM((snaps, snaps), BF16),
            pltpu.VMEM((xl, yl, 4, snaps, cz), BF16),
            dma((xl,)),
        ],
        compiler_params=pltpu.CompilerParams(
            dimension_semantics=("arbitrary",), vmem_limit_bytes=VMEM_LIMIT
        ),
        name="factor_modes",
    )(gram, stack)


def solution(mesh):
    across = mesh.shape["cross"]
    nz = 4 if across >= 32 else 2
    sizes = (mesh.shape["stream"], across // (2 * nz), nz)
    return jax.shard_map(
        functools.partial(shards, sizes),
        mesh=mesh,
        in_specs=(P(None, None, "stream", "cross", None), P("stream"), P("cross"), P()),
        out_specs=(P(None, None, "stream", "cross", None), P()),
        check_vma=False,
    )
```
